512 devices in a mesh: hosp: 32 (over z_hi, y, core), seq: 16 (over z_lo, x).
Axes of the slice: x: 4, y: 8, z: 8 (z_hi: 2, z_lo: 4; z = z_hi * 4 + z_lo), core: 2. Of those that a mesh axis runs over, the one named last changes fastest.
Arguments:
- frames: bfloat16 [32, 8192, 512], P('hosp', 'seq'), may hold values from -6 to 6
- cotangent: bfloat16 [32, 8192, 512], P('hosp', 'seq'), may hold values from -6 to 6
- first_filter: bfloat16 [3, 512, 512], replicated, may hold values from -0.15625 to 0.15625
- second_filter: bfloat16 [3, 512, 512], replicated, may hold values from -0.15625 to 0.15625
Outputs:
- input_gradient: bfloat16 [32, 8192, 512], P('hosp', 'seq')
- grad_one: float32 [512, 3, 512], P('seq', None, 'hosp')
- grad_two: float32 [512, 3, 512], P('seq', None, 'hosp')
The draws below stay inside these ranges and needn't reach their ends.
All inputs are finite; a program needn't handle non-finite values.
Results may differ from the reference program's by a relative error of at most 0.017.
Values may be sent and summed in bfloat16 or wider, within the bound.
A program may use at most 64 MiB of HBM per device.

```python
from functools import partial
import jax
import jax.numpy as jnp
from jax import lax

C = 512
T_DEV = 512
FIRST_DILATION = 512
SECOND_DILATION = 1024
LEN = 8192
GROUPS = 32
N_SEQ = 16


def raised(drawn, stream_key, source, target, blocks, factor):
    owner, partner = [(jnp.arange(drawn.shape[axis_at]) // (drawn.shape[axis_at] // blocks)).reshape([-1 if axis == axis_at else 1 for axis in range(drawn.ndim)]) for axis_at in (source, target)]
    chosen = jax.random.permutation(stream_key, blocks)[partner]
    strong = (owner == chosen) | (owner == (partner + blocks // 2) % blocks)
    return jnp.where(strong, factor * drawn, drawn)


def level_of(key, shape, shards, smallest, top_value):
    loudness, own = 1.0, jax.random.fold_in(key, 6)
    for dim, blocks in shards:
        heights = jnp.exp(jax.random.uniform(jax.random.fold_in(own, dim), (blocks,), jnp.float32, smallest / len(shards), top_value / len(shards)))
        loudness = loudness * jnp.repeat(heights, shape[dim] // blocks).reshape([-1 if axis == dim else 1 for axis in range(len(shape))])
    return loudness


def centred(own_key, shape, deviation, most, split=(), held_as=jnp.bfloat16):
    array = jax.random.normal(own_key, shape, jnp.float32) * deviation
    if len(split) > 0:
        array = level_of(own_key, shape, split, -0.22, 0.18) * array
    return jnp.clip(array, min=-most, max=most).astype(held_as)


def bell_draw_with(rng, dims, scale, most, pieces, heavy, dtype=jnp.bfloat16):
    result = scale * jax.random.normal(rng, dims, jnp.float32)
    if pieces:
        result = result * level_of(rng, dims, pieces, -0.22, 0.18)
    return jnp.clip(raised(result, jax.random.fold_in(rng, 3), *heavy), -most, most).astype(dtype)


def setup_inputs(seed: int = 0) -> dict:
    seeds = jax.random.split(jax.random.key(seed), 5)
    return {
        "frames": centred(seeds[0], (GROUPS, LEN, C), 1.0, 6.0, ((0, 32), (1, 16))),
        "cotangent": bell_draw_with(seeds[1], (GROUPS, LEN, C), 1.0, 6.0, ((0, 32), (1, 16)), (0, 2, 32, 2.75)),
        "first_filter": centred(seeds[2], (3, C, C), (3 * C) ** -0.5, 0.15625),
        "second_filter": centred(seeds[3], (3, C, C), (3 * C) ** -0.5, 0.15625),
    }


def past(v, s):
    return jnp.pad(v, ((s, 0), (0, 0)))[:v.shape[0]]

def ahead(v, s):
    return jnp.pad(v, ((0, s), (0, 0)))[s:]

def silu_grad(v):
    s = jax.nn.sigmoid(v)
    return s * (1.0 + v * (1.0 - s))

def previous_taps(v, d):
    return jnp.stack([v, past(v, d), past(v, 2 * d)], axis=1)

def forward_taps(v, d):
    return jnp.stack([v, ahead(v, d), ahead(v, 2 * d)], axis=1)

def conv(stack, w):
    return jnp.dot(stack.reshape(stack.shape[0], 3 * C), w.reshape(3 * C, C), preferred_element_type=jnp.float32)

def convolution_backward(stack, w):
    wt = jnp.transpose(w, (0, 2, 1)).reshape(3 * C, C)
    return jnp.dot(stack.reshape(stack.shape[0], 3 * C), wt, preferred_element_type=jnp.float32)

def block_terms(stack, delta):
    xs = stack.reshape(N_SEQ, T_DEV, 3, C).astype(jnp.float32)
    ds = delta.reshape(N_SEQ, T_DEV, C).astype(jnp.float32)
    parts = jnp.einsum('btki,bto->biko', xs, ds)
    parts = lax.optimization_barrier(parts.astype(jnp.bfloat16))
    return lax.optimization_barrier(jnp.sum(parts.astype(jnp.float32), axis=0))

def one_group(first_filter, second_filter, carry, item):
    input_frames, output_gradient = item
    acc_one, acc_two = carry
    first_stack = previous_taps(input_frames, FIRST_DILATION)
    pre_one = conv(first_stack, first_filter)
    hidden_state = (input_frames.astype(jnp.float32) + jax.nn.silu(pre_one)).astype(jnp.bfloat16)
    second_stack = previous_taps(hidden_state, SECOND_DILATION)
    pre_two = conv(second_stack, second_filter)
    second_delta = (output_gradient.astype(jnp.float32) * silu_grad(pre_two)).astype(jnp.bfloat16)
    hidden_gradient = output_gradient.astype(jnp.float32) + convolution_backward(forward_taps(second_delta, SECOND_DILATION), second_filter)
    first_delta = (hidden_gradient * silu_grad(pre_one)).astype(jnp.bfloat16)
    input_gradient = (hidden_gradient + convolution_backward(forward_taps(first_delta, FIRST_DILATION), first_filter)).astype(jnp.bfloat16)
    acc_one = acc_one + block_terms(first_stack, first_delta)
    acc_two = acc_two + block_terms(second_stack, second_delta)
    return ((acc_one, acc_two), input_gradient)

def reference(frames, cotangent, first_filter, second_filter):
    start = (jnp.zeros((C, 3, C), jnp.float32), jnp.zeros((C, 3, C), jnp.float32))
    stepper = partial(one_group, first_filter, second_filter)
    (acc_one, acc_two), input_gradient = lax.scan(stepper, start, (frames, cotangent))
    scale = 1.0 / jnp.sqrt(jnp.float32(GROUPS * LEN))
    return (input_gradient, acc_one * scale, acc_two * scale)
```

```python
import math

import jax
import jax.numpy as jnp
from jax import lax
from jax.sharding import PartitionSpec as P

FIRST_DILATION = 512
SECOND_DILATION = 1024
BF = jnp.bfloat16
F32 = jnp.float32


def silu_grad(value):
    sigma = jax.nn.sigmoid(value)
    return sigma * (1.0 + value * (1.0 - sigma))


def regroup(block, n):
    rows, channels = block.shape
    parts = block.reshape(n, rows // n, channels)
    return lax.all_to_all(parts, "seq", 0, 0).reshape(rows, channels)


def past(v, s):
    return jnp.concatenate([jnp.zeros((s, v.shape[1]), v.dtype), v[: v.shape[0] - s]], axis=0)


def ahead(v, s):
    return jnp.concatenate([v[s:], jnp.zeros((s, v.shape[1]), v.dtype)], axis=0)


def dot(a, b):
    return jnp.dot(a, b, preferred_element_type=F32)


def conv(v, w, s):
    return dot(v, w[0]) + dot(past(v, s), w[1]) + dot(past(v, 2 * s), w[2])


def conv_back(d, w, s):
    total = None
    for k in range(3):
        term = lax.dot_general(
            d if k == 0 else ahead(d, k * s), w[k], (((1,), (1,)), ((), ())),
            preferred_element_type=F32,
        )
        total = term if total is None else total + term
    return total


def filter_share(v, delta, s, mine, n_seq, n_hosp):
    channels = v.shape[1]
    turned = dot(delta, mine).astype(BF)
    terms = jnp.stack(
        [
            lax.dot_general(
                v if k == 0 else past(v, k * s), turned, (((0,), (0,)), ((), ())),
                preferred_element_type=F32,
            )
            for k in range(3)
        ]
    )
    half = channels // 2
    swap = [(i, i ^ 1) for i in range(n_hosp)]
    other = lax.ppermute(terms[:, :, half:].astype(BF), "hosp", swap)
    pair = (terms[:, :, :half] + other.astype(F32)).astype(BF)
    depth = channels // n_seq
    pair = pair.reshape(3, n_seq, depth, half).transpose(1, 0, 2, 3)
    pair = lax.all_to_all(pair, "seq", 0, 0)
    return jnp.sum(pair.astype(F32), axis=0).astype(BF)


def per_device(frames, cotangent, first_filter, second_filter):
    n_seq = lax.axis_size("seq")
    n_hosp = lax.axis_size("hosp")
    rows, channels = frames.shape[1:]
    s1 = FIRST_DILATION // n_seq
    s2 = SECOND_DILATION // n_seq
    inputs = regroup(frames[0], n_seq)
    upstream = regroup(cotangent[0], n_seq).astype(F32)

    core = lax.axis_index("hosp") % 2
    width = channels // n_hosp
    half = channels // 2
    j = jnp.arange(channels)
    jj = j % half
    source = (jj // width) * (2 * width) + jnp.where(j < half, core, 1 - core) * width + jj % width
    mine = (jnp.arange(channels)[:, None] == source[None, :]).astype(BF)

    pre_one = conv(inputs, first_filter, s1)
    hidden = (inputs.astype(F32) + jax.nn.silu(pre_one)).astype(BF)
    pre_two = conv(hidden, second_filter, s2)
    second_delta = (upstream * silu_grad(pre_two)).astype(BF)
    hidden_grad = upstream + conv_back(second_delta, second_filter, s2)
    first_delta = (hidden_grad * silu_grad(pre_one)).astype(BF)
    input_grad = (hidden_grad + conv_back(first_delta, first_filter, s1)).astype(BF)
    input_grad = regroup(input_grad, n_seq)

    two = filter_share(hidden, second_delta, s2, mine, n_seq, n_hosp)
    one = filter_share(inputs, first_delta, s1, mine, n_seq, n_hosp)
    depth = channels // n_seq
    pieces = n_hosp // 2
    both = jnp.concatenate([one, two], axis=0).reshape(6, depth, pieces, width)
    both = both.transpose(2, 0, 1, 3)
    same_core = [[2 * p + c for p in range(pieces)] for c in range(2)]
    both = lax.all_to_all(both, "hosp", 0, 0, axis_index_groups=same_core)
    both = jnp.sum(both.astype(F32), axis=0)
    both = both * (1.0 / math.sqrt(n_hosp * rows * n_seq))
    both = both.transpose(1, 0, 2)
    return (input_grad[None], both[:, :3], both[:, 3:])


def solution(mesh):
    in_specs = (P("hosp", "seq", None), P("hosp", "seq", None), P(), P())
    out_specs = (P("hosp", "seq", None), P("seq", None, "hosp"), P("seq", None, "hosp"))
    return jax.shard_map(
        per_device, mesh=mesh, in_specs=in_specs, out_specs=out_specs, check_vma=False
    )
```

```python
import math

import jax
import jax.numpy as jnp
from jax import lax
from jax.experimental import pallas as pl
from jax.experimental.pallas import tpu as pltpu
from jax.sharding import PartitionSpec as P

FIRST_DILATION = 512
SECOND_DILATION = 1024
BF = jnp.bfloat16
F32 = jnp.float32
ZH, NY, NC, ZL, NX = 2, 8, 2, 4, 4
NS = ZL * NX
NZ = ZH * ZL
C = 512
R = 512
SUB = R // NS
S1 = FIRST_DILATION // NS
S2 = SECOND_DILATION // NS
HALF = C // NC
YW = HALF // NY
ZW = YW // ZH
XW = C // NX
STEP = 256


def silu_grad(value):
    sigma = jax.nn.sigmoid(value)
    return sigma * (1.0 + value * (1.0 - sigma))


def nn(a, b):
    return jnp.dot(a, b, preferred_element_type=F32)


def nt(a, b):
    return lax.dot_general(a, b, (((1,), (1,)), ((), ())), preferred_element_type=F32)


def over_rows(body):
    def step(c, carry):
        body(pl.multiple_of(c * STEP, STEP))
        return carry

    lax.fori_loop(0, R // STEP, step, 0)


def kernel(
    frames, cot, w1, w2, perm_i, perm_o,
    out, grads,
    fp, hp, fq, hq, d1, d2, cots, g1, g2, hg, ig, tt,
    mine, other, got, s0, ry2, sx2, rx2, rx1, sy1, ry1, s2, rz,
    sem_f, sem_c, sem_g, sem_w, sem_y2, sem_x2, sem_x1, sem_y1, sem_z,
):
    h = lax.axis_index("hosp")
    s = lax.axis_index("seq")
    core = lax.rem(h, NC)
    y = lax.rem(lax.div(h, NC), NY)
    zh = lax.div(h, NC * NY)
    x = lax.rem(s, NX)
    zl = lax.div(s, NX)
    z = zh * ZL + zl

    def seq_dev(t):
        return (h, t)

    def x_dev(t):
        return (h, zl * NX + t)

    def y_dev(t):
        return ((zh * NY + t) * NC + core, s)

    def z_dev(t):
        return ((lax.div(t, ZL) * NY + y) * NC + core, lax.rem(t, ZL) * NX + x)

    partner = (h + 1 - 2 * core, s)
    barrier = pltpu.get_barrier_semaphore()

    def greet(dev):
        pl.semaphore_signal(barrier, inc=1, device_id=dev, device_id_type=pl.DeviceIdType.MESH)

    def loop(first, last, body):
        def step(r, carry):
            body(r)
            return carry

        lax.fori_loop(first, last, step, 0)

    loop(1, NS, lambda r: greet(seq_dev(lax.rem(s + r, NS))))
    loop(1, NY, lambda r: greet(y_dev(lax.rem(y + r, NY))))
    loop(0, ZL, lambda r: greet(z_dev((1 - zh) * ZL + r)))
    greet(partner)
    pl.semaphore_wait(barrier, NS - 1 + NY - 1 + ZL + 1)

    class Exchange:
        def __init__(self, n, me, dev, src, dst, sem):
            self.n, self.me, self.dev, self.src, self.dst, self.sem = n, me, dev, src, dst, sem

        def copy(self, r, to, slot):
            return pltpu.make_async_remote_copy(
                src_ref=self.src(to), dst_ref=self.dst(slot),
                send_sem=self.sem.at[0, r], recv_sem=self.sem.at[1, r],
                device_id=self.dev(to), device_id_type=pl.DeviceIdType.MESH,
            )

        def push(self):
            loop(1, self.n, lambda r: self.copy(r, lax.rem(self.me + r, self.n), self.me).start())

        def land(self):
            def body(r):
                slot = lax.rem(self.me + self.n - r, self.n)
                self.copy(r, lax.rem(self.me + r, self.n), slot).wait_recv()

            loop(1, self.n, body)

        def sent(self):
            loop(1, self.n, lambda r: self.copy(r, lax.rem(self.me + r, self.n), self.me).wait_send())

    def rows_at(base):
        return lambda t: pl.ds(pl.multiple_of(base + t * SUB, SUB), SUB)

    at_f = rows_at(2 * S1)
    at_0 = rows_at(0)
    ex_f = Exchange(NS, s, seq_dev, lambda t: frames.at[at_0(t)], lambda t: fp.at[at_f(t)], sem_f)
    ex_c = Exchange(NS, s, seq_dev, lambda t: cot.at[at_0(t)], lambda t: cots.at[at_0(t)], sem_c)
    ex_g = Exchange(NS, s, seq_dev, lambda t: ig.at[at_0(t)], lambda t: out.at[at_0(t)], sem_g)

    def at_y(t):
        return pl.ds(pl.multiple_of(t * YW, YW), YW)

    def at_x(t):
        return pl.ds(pl.multiple_of(t * XW, XW), XW)

    def at_z(t):
        return pl.ds(pl.multiple_of(lax.div(t, ZL) * ZW, ZW), ZW)

    ex_y2 = Exchange(NY, y, y_dev, lambda t: s0.at[1, :, at_y(t), :], lambda t: ry2.at[t], sem_y2)
    ex_x2 = Exchange(NX, x, x_dev, lambda t: sx2.at[:, :, at_x(t)], lambda t: rx2.at[t], sem_x2)
    ex_x1 = Exchange(NX, x, x_dev, lambda t: s0.at[0, :, :, at_x(t)], lambda t: rx1.at[t], sem_x1)
    ex_y1 = Exchange(NY, y, y_dev, lambda t: sy1.at[:, at_y(t), :], lambda t: ry1.at[t], sem_y1)
    ex_z = Exchange(NZ, z, z_dev, lambda t: s2.at[:, at_z(t), :], lambda t: rz.at[t], sem_z)

    ex_f.push()
    ex_c.push()

    fp[0 : 2 * S1, :] = jnp.zeros((2 * S1, C), BF)
    fq[0 : 2 * S1, :] = jnp.zeros((2 * S1, C), BF)
    hp[0 : 2 * S2, :] = jnp.zeros((2 * S2, C), BF)
    hq[0 : 2 * S2, :] = jnp.zeros((2 * S2, C), BF)
    d1[R : R + 2 * S1, :] = jnp.zeros((2 * S1, C), BF)
    d2[R : R + 2 * S2, :] = jnp.zeros((2 * S2, C), BF)
    fp[at_f(s), :] = frames[at_0(s), :]
    cots[at_0(s), :] = cot[at_0(s), :]

    def rows(ref, start, size=STEP):
        return ref[pl.ds(pl.multiple_of(start, SUB), size), :]

    def put(ref, start, value):
        ref[pl.ds(pl.multiple_of(start, SUB), STEP), :] = value

    ex_f.land()

    def forward_one(c):
        base = 2 * S1 + c
        here = rows(fp, base)
        pre = nn(here, w1[0]) + nn(rows(fp, base - S1), w1[1]) + nn(rows(fp, base - 2 * S1), w1[2])
        sigma = jax.nn.sigmoid(pre)
        put(g1, c, sigma * (1.0 + pre * (1.0 - sigma)))
        put(hp, 2 * S2 + c, (here.astype(F32) + pre * sigma).astype(BF))

    over_rows(forward_one)

    def forward_two(c):
        base = 2 * S2 + c
        pre = (
            nn(rows(hp, base), w2[0]) + nn(rows(hp, base - S2), w2[1])
            + nn(rows(hp, base - 2 * S2), w2[2])
        )
        put(g2, c, silu_grad(pre))

    over_rows(forward_two)

    def reorder(c):
        put(fq, 2 * S1 + c, nn(rows(fp, 2 * S1 + c), perm_i[...]).astype(BF))
        put(hq, 2 * S2 + c, nn(rows(hp, 2 * S2 + c), perm_i[...]).astype(BF))

    over_rows(reorder)

    ex_c.land()

    def second_delta(c):
        put(d2, c, (rows(cots, c).astype(F32) * rows(g2, c)).astype(BF))

    over_rows(second_delta)

    def swap(layer, k):
        return pltpu.make_async_remote_copy(
            src_ref=other.at[layer, k], dst_ref=got.at[layer, k],
            send_sem=sem_w.at[0, layer, k], recv_sem=sem_w.at[1, layer, k],
            device_id=partner, device_id_type=pl.DeviceIdType.MESH,
        )

    def terms(layer, delta, source, pad, shift):
        def turn(c):
            put(tt, c, nt(rows(perm_o, c), delta[0:R, :]).astype(BF))

        over_rows(turn)

        def theirs(k):
            taps = rows(source, pad - k * shift, R)
            other[layer, k] = nn(tt[HALF:, :], taps).astype(BF)
            swap(layer, k).start()

        loop(0, 3, theirs)

        def ours(k):
            mine[k] = nn(tt[:HALF, :], rows(source, pad - k * shift, R))

        loop(0, 3, ours)

    def pair_sum(layer):
        def one(k):
            swap(layer, k).wait_recv()
            s0[layer, k] = (mine[k] + got[layer, k].astype(F32)).astype(BF)

        loop(0, 3, one)

    terms(1, d2, hq, 2 * S2, S2)
    pair_sum(1)
    ex_y2.push()

    def first_delta(c):
        value = (
            rows(cots, c).astype(F32) + nt(rows(d2, c), w2[0]) + nt(rows(d2, c + S2), w2[1])
            + nt(rows(d2, c + 2 * S2), w2[2])
        )
        put(hg, c, value)
        put(d1, c, (value * rows(g1, c)).astype(BF))

    over_rows(first_delta)
    terms(0, d1, fq, 2 * S1, S1)

    def input_grad(c):
        value = (
            rows(hg, c) + nt(rows(d1, c), w1[0]) + nt(rows(d1, c + S1), w1[1])
            + nt(rows(d1, c + 2 * S1), w1[2])
        )
        put(ig, c, value.astype(BF))

    pair_sum(0)
    ex_x1.push()
    over_rows(input_grad)
    ex_g.push()
    out[at_0(s), :] = ig[at_0(s), :]

    def gather(ex, own, n, me):
        ex.dst(me)[...] = own
        ex.land()
        ref = ex.dst
        total = ref(0)[...].astype(F32)
        for t in range(1, n):
            total = total + ref(t)[...].astype(F32)
        return total

    sx2[...] = gather(ex_y2, s0[1, :, at_y(y), :], NY, y).astype(BF)
    ex_x2.push()
    sy1[...] = gather(ex_x1, s0[0, :, :, at_x(x)], NX, x).astype(BF)
    ex_y1.push()
    s2[3:6] = gather(ex_x2, sx2[:, :, at_x(x)], NX, x).astype(BF)
    s2[0:3] = gather(ex_y1, sy1[:, at_y(y), :], NY, y).astype(BF)
    ex_z.push()
    grads[...] = gather(ex_z, s2[:, at_z(z), :], NZ, z)
    ex_g.land()

    for ex in (ex_f, ex_c, ex_g, ex_y2, ex_x2, ex_x1, ex_y1, ex_z):
        ex.sent()
    loop(0, 3, lambda k: swap(0, k).wait_send())
    loop(0, 3, lambda k: swap(1, k).wait_send())


def per_device(frames, cotangent, first_filter, second_filter):
    core = lax.axis_index("hosp") % NC
    zl = lax.axis_index("seq") // NX
    a = jnp.arange(C)
    width = C // NS
    i_from = ((a // width) % ZL) * (NX * width) + (a // (ZL * width)) * width + a % width
    perm_i = (a[:, None] == i_from[None, :]).astype(BF)
    owner = jnp.where(a < HALF, core, 1 - core)
    b = a % HALF
    o_from = ((b // ZW) % ZH) * (NY * NC * ZW) + (b // YW) * (NC * ZW) + owner * ZW + b % ZW
    perm_o = (o_from[:, None] == a[None, :]).astype(BF)

    vmem = pl.BlockSpec(memory_space=pltpu.VMEM)
    dma = pltpu.SemaphoreType.DMA
    out, grads = pl.pallas_call(
        kernel,
        out_shape=(
            jax.ShapeDtypeStruct((R, C), BF),
            jax.ShapeDtypeStruct((6, ZW, XW), F32),
        ),
        in_specs=[vmem] * 6,
        out_specs=(vmem, vmem),
        scratch_shapes=[
            pltpu.VMEM((R + 2 * S1, C), BF),
            pltpu.VMEM((R + 2 * S2, C), BF),
            pltpu.VMEM((R + 2 * S1, C), BF),
            pltpu.VMEM((R + 2 * S2, C), BF),
            pltpu.VMEM((R + 2 * S1, C), BF),
            pltpu.VMEM((R + 2 * S2, C), BF),
            pltpu.VMEM((R, C), BF),
            pltpu.VMEM((R, C), F32),
            pltpu.VMEM((R, C), F32),
            pltpu.VMEM((R, C), F32),
            pltpu.VMEM((R, C), BF),
            pltpu.VMEM((C, R), BF),
            pltpu.VMEM((3, HALF, C), F32),
            pltpu.VMEM((2, 3, HALF, C), BF),
            pltpu.VMEM((2, 3, HALF, C), BF),
            pltpu.VMEM((2, 3, HALF, C), BF),
            pltpu.VMEM((NY, 3, YW, C), BF),
            pltpu.VMEM((3, YW, C), BF),
            pltpu.VMEM((NX, 3, YW, XW), BF),
            pltpu.VMEM((NX, 3, HALF, XW), BF),
            pltpu.VMEM((3, HALF, XW), BF),
            pltpu.VMEM((NY, 3, YW, XW), BF),
            pltpu.VMEM((6, YW, XW), BF),
            pltpu.VMEM((NZ, 6, ZW, XW), BF),
            dma((2, NS)),
            dma((2, NS)),
            dma((2, NS)),
            dma((2, 2, 3)),
            dma((2, NY)),
            dma((2, NX)),
            dma((2, NX)),
            dma((2, NY)),
            dma((2, NZ)),
        ],
        compiler_params=pltpu.CompilerParams(
            collective_id=0, has_side_effects=True, vmem_limit_bytes=48 * 1024 * 1024
        ),
    )(frames[0], cotangent[0], first_filter, second_filter, perm_i, perm_o)
    scale = 1.0 / math.sqrt(lax.axis_size("hosp") * R * lax.axis_size("seq"))
    own = lax.dynamic_slice_in_dim(grads, zl * width, width, axis=2) * scale
    own = own.transpose(2, 0, 1)
    return (out[None], own[:, :3], own[:, 3:])


def solution(mesh):
    in_specs = (P("hosp", "seq", None), P("hosp", "seq", None), P(), P())
    out_specs = (P("hosp", "seq", None), P("seq", None, "hosp"), P("seq", None, "hosp"))
    return jax.shard_map(
        per_device, mesh=mesh, in_specs=in_specs, out_specs=out_specs, check_vma=False
    )
```

```python
import math

import jax
import jax.numpy as jnp
from jax import lax
from jax.experimental import pallas as pl
from jax.experimental.pallas import tpu as pltpu
from jax.sharding import PartitionSpec as P

FIRST_DILATION = 512
SECOND_DILATION = 1024
BF = jnp.bfloat16
F32 = jnp.float32
ZH, NY, NC, ZL, NX = 2, 8, 2, 4, 4
NS = ZL * NX
NZ = ZH * ZL
C = 512
R = 512
PARTS = 1
M = R // PARTS
SUB = M // NS
S1 = FIRST_DILATION // NS // PARTS
S2 = SECOND_DILATION // NS // PARTS
HALF = C // NC
YW = HALF // NY
ZW = YW // ZH
XW = C // NX


def silu_grad(value):
    sigma = jax.nn.sigmoid(value)
    return sigma * (1.0 + value * (1.0 - sigma))


def nn(a, b):
    return jnp.dot(a, b, preferred_element_type=F32)


def nt(a, b):
    return lax.dot_general(a, b, (((1,), (1,)), ((), ())), preferred_element_type=F32)


def kernel(
    frames, cot, first, second, perm_i, perm_o,
    out, grads,
    fp, hp, fq, hq, d1, d2, cots, g1, g2, hg, ig, tt,
    acc, other, got, s0, sx, rx, sy, ry, s2, rz,
    w1, w2, w1t, w2t, sem_l,
    sem_f, sem_c, sem_g, sem_w, sem_x, sem_y, sem_z,
):
    h = lax.axis_index("hosp")
    s = lax.axis_index("seq")
    core = lax.rem(h, NC)
    y = lax.rem(lax.div(h, NC), NY)
    zh = lax.div(h, NC * NY)
    x = lax.rem(s, NX)
    zl = lax.div(s, NX)
    z = zh * ZL + zl

    def seq_dev(t):
        return (h, t)

    def x_dev(t):
        return (h, zl * NX + t)

    def y_dev(t):
        return ((zh * NY + t) * NC + core, s)

    def z_dev(t):
        return ((lax.div(t, ZL) * NY + y) * NC + core, lax.rem(t, ZL) * NX + x)

    partner = (h + 1 - 2 * core, s)
    loads = [
        pltpu.make_async_copy(src, dst, sem_l.at[i])
        for i, (src, dst) in enumerate(
            ((first, w1), (second, w2))
        )
    ]

    def at_part(t):
        return pl.ds(pl.multiple_of(t * SUB, SUB), SUB)

    def at_pad(t):
        return pl.ds(pl.multiple_of(2 * S1 + t * SUB, SUB), SUB)

    def at_full(p):
        return lambda t: pl.ds(pl.multiple_of(t * (PARTS * SUB) + p * SUB, SUB), SUB)

    own_f = [
        pltpu.make_async_copy(
            frames.at[at_full(p)(s)], fp.at[p, at_pad(s)], sem_l.at[4 + p]
        )
        for p in range(PARTS)
    ]
    own_c = [
        pltpu.make_async_copy(
            cot.at[at_full(p)(s)], cots.at[p, at_part(s)], sem_l.at[6 + p]
        )
        for p in range(PARTS)
    ]
    barrier = pltpu.get_barrier_semaphore()

    def greet(dev):
        pl.semaphore_signal(barrier, inc=1, device_id=dev, device_id_type=pl.DeviceIdType.MESH)

    def loop(first, last, body):
        def step(r, carry):
            body(r)
            return carry

        lax.fori_loop(first, last, step, 0)

    loop(1, NS, lambda r: greet(seq_dev(lax.rem(s + r, NS))))
    loop(1, NY, lambda r: greet(y_dev(lax.rem(y + r, NY))))
    loop(0, ZL, lambda r: greet(z_dev((1 - zh) * ZL + r)))
    greet(partner)
    pl.semaphore_wait(barrier, NS - 1 + NY - 1 + ZL + 1)

    class Exchange:
        def __init__(self, n, me, dev, src, dst, sem):
            self.n, self.me, self.dev, self.src, self.dst, self.sem = n, me, dev, src, dst, sem

        def copy(self, r, to, slot):
            return pltpu.make_async_remote_copy(
                src_ref=self.src(to), dst_ref=self.dst(slot),
                send_sem=self.sem.at[0, r], recv_sem=self.sem.at[1, r],
                device_id=self.dev(to), device_id_type=pl.DeviceIdType.MESH,
            )

        def push(self):
            loop(1, self.n, lambda r: self.copy(r, lax.rem(self.me + r, self.n), self.me).start())

        def land(self):
            def body(r):
                slot = lax.rem(self.me + self.n - r, self.n)
                self.copy(r, lax.rem(self.me + r, self.n), slot).wait_recv()

            loop(1, self.n, body)

        def sent(self):
            loop(1, self.n, lambda r: self.copy(r, lax.rem(self.me + r, self.n), self.me).wait_send())

    ex_f = [
        Exchange(NS, s, seq_dev, lambda t, p=p: frames.at[at_full(p)(t)],
                 lambda t, p=p: fp.at[p, at_pad(t)], sem_f.at[p])
        for p in range(PARTS)
    ]
    ex_c = [
        Exchange(NS, s, seq_dev, lambda t, p=p: cot.at[at_full(p)(t)],
                 lambda t, p=p: cots.at[p, at_part(t)], sem_c.at[p])
        for p in range(PARTS)
    ]
    ex_g = [
        Exchange(NS, s, seq_dev, lambda t, p=p: ig.at[p, at_part(t)],
                 lambda t, p=p: out.at[at_full(p)(t)], sem_g.at[p])
        for p in range(PARTS)
    ]

    def at_y(t):
        return pl.ds(pl.multiple_of(t * YW, YW), YW)

    def at_x(t):
        return pl.ds(pl.multiple_of(t * XW, XW), XW)

    def at_z(t):
        return pl.ds(pl.multiple_of(lax.div(t, ZL) * ZW, ZW), ZW)

    def y_stage(layer):
        return Exchange(
            NY, y, y_dev, lambda t: sy.at[layer, :, at_y(t), :], lambda t: ry.at[layer, t],
            sem_y.at[layer],
        )

    ex_y = (y_stage(0), y_stage(1))
    ex_z = Exchange(NZ, z, z_dev, lambda t: s2.at[:, at_z(t), :], lambda t: rz.at[t], sem_z)

    for p in range(PARTS):
        ex_f[p].push()
        ex_c[p].push()
        if p == 0:
            for load in (*loads, *own_f, *own_c):
                load.start()

    for p in range(PARTS):
        fp[p, 0 : 2 * S1, :] = jnp.zeros((2 * S1, C), BF)
        fq[p, 0 : 2 * S1, :] = jnp.zeros((2 * S1, C), BF)
        hp[p, 0 : 2 * S2, :] = jnp.zeros((2 * S2, C), BF)
        hq[p, 0 : 2 * S2, :] = jnp.zeros((2 * S2, C), BF)
        d1[p, M : M + 2 * S1, :] = jnp.zeros((2 * S1, C), BF)
        d2[p, M : M + 2 * S2, :] = jnp.zeros((2 * S2, C), BF)

    def behind(ref, p, shift):
        return jnp.concatenate([ref[p, j * shift : j * shift + M, :] for j in (2, 1, 0)], axis=1)

    def beyond(ref, p, shift):
        return jnp.concatenate([ref[p, j * shift : j * shift + M, :] for j in (0, 1, 2)], axis=1)

    def forward(p):
        own_f[p].wait()
        ex_f[p].land()
        here = fp[p, 2 * S1 :, :]
        pre = nn(behind(fp, p, S1), w1[...])
        sigma = jax.nn.sigmoid(pre)
        g1[p] = sigma * (1.0 + pre * (1.0 - sigma))
        hp[p, 2 * S2 :, :] = (here.astype(F32) + pre * sigma).astype(BF)
        g2[p] = silu_grad(nn(behind(hp, p, S2), w2[...]))
        fq[p, 2 * S1 :, :] = nn(here, perm_i[...]).astype(BF)
        hq[p, 2 * S2 :, :] = nn(hp[p, 2 * S2 :, :], perm_i[...]).astype(BF)

    def second_delta(p):
        own_c[p].wait()
        ex_c[p].land()
        d2[p, 0:M, :] = (cots[p].astype(F32) * g2[p]).astype(BF)

    def first_delta(p):
        value = cots[p].astype(F32) + nn(beyond(d2, p, S2), w2t[...])
        hg[p] = value
        d1[p, 0:M, :] = (value * g1[p]).astype(BF)

    def input_grad(p):
        ig[p] = (hg[p] + nn(beyond(d1, p, S1), w1t[...])).astype(BF)

    def send_grad(p):
        ex_g[p].push()
        out[at_full(p)(s), :] = ig[p, at_part(s), :]

    def swap(layer, k):
        return pltpu.make_async_remote_copy(
            src_ref=other.at[layer, k], dst_ref=got.at[layer, k],
            send_sem=sem_w.at[0, layer, k], recv_sem=sem_w.at[1, layer, k],
            device_id=partner, device_id_type=pl.DeviceIdType.MESH,
        )

    def taps(source, p, k, shift):
        return source[p, pl.ds(pl.multiple_of((2 - k) * shift, SUB), M), :]

    def turn(delta, p):
        tt[...] = nt(perm_o[...], delta[p, 0:M, :]).astype(BF)

    def terms(layer, delta, source, shift, between):
        turn(delta, 0)

        def theirs(k):
            value = nn(tt[HALF:, :], taps(source, 0, k, shift))
            other[layer, k] = value.astype(BF)
            swap(layer, k).start()

        loop(0, 3, theirs)
        between()

        def ours(k):
            acc[layer, k] = nn(tt[:HALF, :], taps(source, 0, k, shift))

        loop(0, 3, ours)

    def pair_sum(layer):
        def one(k):
            swap(layer, k).wait_recv()
            s0[layer, k] = (acc[layer, k] + got[layer, k].astype(F32)).astype(BF)

        loop(0, 3, one)

    right, left, far = (lax.rem(x + d, NX) for d in (1, NX - 1, NX // 2))
    low, high = pl.ds(0, HALF // 2), pl.ds(HALF // 2, HALF // 2)

    def piece(layer, part, to):
        return s0.at[layer, :, part, at_x(to)]

    def hop(layer, i):
        source = (
            lambda: piece(layer, low, far), lambda: piece(layer, high, far),
            lambda: piece(layer, high, right), lambda: piece(layer, low, left),
            lambda: sx.at[layer, 0], lambda: sx.at[layer, 1],
        )[i]()
        return pltpu.make_async_remote_copy(
            src_ref=source, dst_ref=rx.at[layer, i],
            send_sem=sem_x.at[0, layer, i], recv_sem=sem_x.at[1, layer, i],
            device_id=x_dev(left if i % 2 else right), device_id_type=pl.DeviceIdType.MESH,
        )

    def x_first(layer):
        for i in range(4):
            hop(layer, i).start()

    def x_merge(layer):
        for i, own in ((0, piece(layer, low, right)), (1, piece(layer, high, left))):
            hop(layer, i).wait_recv()
            sx[layer, i] = (own[...].astype(F32) + rx[layer, i].astype(F32)).astype(BF)
            hop(layer, 4 + i).start()

    def x_sum(layer):
        for i in (2, 3, 4, 5):
            hop(layer, i).wait_recv()
        for part, a, b in ((low, 3, 4), (high, 2, 5)):
            total = (
                piece(layer, part, x)[...].astype(F32) + rx[layer, a].astype(F32)
                + rx[layer, b].astype(F32)
            )
            sy[layer, :, part, :] = total.astype(BF)
        ex_y[layer].push()

    unit = lax.broadcasted_iota(jnp.int32, (C, C), 0) == lax.broadcasted_iota(jnp.int32, (C, C), 1)
    unit = unit.astype(F32).astype(BF)
    for load, w, wt in ((loads[0], w1, w1t), (loads[1], w2, w2t)):
        load.wait()
        for k in range(3):
            wt[k * C : (k + 1) * C, :] = nt(unit, w[k * C : (k + 1) * C, :]).astype(BF)

    forward(0)
    second_delta(0)
    terms(1, d2, hq, S2, lambda: None)
    first_delta(0)
    pair_sum(1)
    x_first(1)
    terms(0, d1, fq, S1, lambda: x_merge(1))
    pair_sum(0)
    x_first(0)
    x_sum(1)
    input_grad(0)
    x_merge(0)
    send_grad(0)

    def gather(ex, own, n, me):
        ex.dst(me)[...] = own
        ex.land()
        ref = ex.dst
        total = ref(0)[...].astype(F32)
        for t in range(1, n):
            total = total + ref(t)[...].astype(F32)
        return total

    x_sum(0)
    s2[3:6] = gather(ex_y[1], sy[1, :, at_y(y), :], NY, y).astype(BF)
    s2[0:3] = gather(ex_y[0], sy[0, :, at_y(y), :], NY, y).astype(BF)
    ex_z.push()
    grads[...] = gather(ex_z, s2[:, at_z(z), :], NZ, z)
    ex_g[0].land()

    for ex in (*ex_f, *ex_c, *ex_g, *ex_y, ex_z):
        ex.sent()
    for i in range(6):
        hop(0, i).wait_send()
        hop(1, i).wait_send()
    loop(0, 3, lambda k: swap(0, k).wait_send())
    loop(0, 3, lambda k: swap(1, k).wait_send())


def per_device(frames, cotangent, first_filter, second_filter):
    core = lax.axis_index("hosp") % NC
    zl = lax.axis_index("seq") // NX
    a = jnp.arange(C)
    width = C // NS
    i_from = ((a // width) % ZL) * (NX * width) + (a // (ZL * width)) * width + a % width
    perm_i = (a[:, None] == i_from[None, :]).astype(BF)
    owner = jnp.where(a < HALF, core, 1 - core)
    b = a % HALF
    o_from = ((b // ZW) % ZH) * (NY * NC * ZW) + (b // YW) * (NC * ZW) + owner * ZW + b % ZW
    perm_o = (o_from[:, None] == a[None, :]).astype(BF)

    vmem = pl.BlockSpec(memory_space=pltpu.VMEM)
    hbm = pl.BlockSpec(memory_space=pltpu.HBM)
    dma = pltpu.SemaphoreType.DMA
    out, grads = pl.pallas_call(
        kernel,
        out_shape=(
            jax.ShapeDtypeStruct((R, C), BF),
            jax.ShapeDtypeStruct((6, ZW, XW), F32),
        ),
        in_specs=[hbm] * 4 + [vmem] * 2,
        out_specs=(vmem, vmem),
        scratch_shapes=[
            pltpu.VMEM((PARTS, M + 2 * S1, C), BF),
            pltpu.VMEM((PARTS, M + 2 * S2, C), BF),
            pltpu.VMEM((PARTS, M + 2 * S1, C), BF),
            pltpu.VMEM((PARTS, M + 2 * S2, C), BF),
            pltpu.VMEM((PARTS, M + 2 * S1, C), BF),
            pltpu.VMEM((PARTS, M + 2 * S2, C), BF),
            pltpu.VMEM((PARTS, M, C), BF),
            pltpu.VMEM((PARTS, M, C), F32),
            pltpu.VMEM((PARTS, M, C), F32),
            pltpu.VMEM((PARTS, M, C), F32),
            pltpu.VMEM((PARTS, M, C), BF),
            pltpu.VMEM((C, M), BF),
            pltpu.VMEM((2, 3, HALF, C), F32),
            pltpu.VMEM((2, 3, HALF, C), BF),
            pltpu.VMEM((2, 3, HALF, C), BF),
            pltpu.VMEM((2, 3, HALF, C), BF),
            pltpu.VMEM((2, 2, 3, HALF // 2, XW), BF),
            pltpu.VMEM((2, 6, 3, HALF // 2, XW), BF),
            pltpu.VMEM((2, 3, HALF, XW), BF),
            pltpu.VMEM((2, NY, 3, YW, XW), BF),
            pltpu.VMEM((6, YW, XW), BF),
            pltpu.VMEM((NZ, 6, ZW, XW), BF),
            pltpu.VMEM((3 * C, C), BF),
            pltpu.VMEM((3 * C, C), BF),
            pltpu.VMEM((3 * C, C), BF),
            pltpu.VMEM((3 * C, C), BF),
            dma((8,)),
            dma((PARTS, 2, NS)),
            dma((PARTS, 2, NS)),
            dma((PARTS, 2, NS)),
            dma((2, 2, 3)),
            dma((2, 2, 6)),
            dma((2, 2, NY)),
            dma((2, NZ)),
        ],
        compiler_params=pltpu.CompilerParams(
            collective_id=0, has_side_effects=True, vmem_limit_bytes=56 * 1024 * 1024
        ),
    )(
        frames[0], cotangent[0],
        first_filter.reshape(3 * C, C), second_filter.reshape(3 * C, C),
        perm_i, perm_o,
    )
    scale = 1.0 / math.sqrt(lax.axis_size("hosp") * R * lax.axis_size("seq"))
    own = lax.dynamic_slice_in_dim(grads, zl * width, width, axis=2) * scale
    own = own.transpose(2, 0, 1)
    return (out[None], own[:, :3], own[:, 3:])


def solution(mesh):
    in_specs = (P("hosp", "seq", None), P("hosp", "seq", None), P(), P())
    out_specs = (P("hosp", "seq", None), P("seq", None, "hosp"), P("seq", None, "hosp"))
    return jax.shard_map(
        per_device, mesh=mesh, in_specs=in_specs, out_specs=out_specs, check_vma=False
    )
```

```python
import math

import jax
import jax.numpy as jnp
from jax import lax
from jax.experimental import pallas as pl
from jax.experimental.pallas import tpu as pltpu
from jax.sharding import PartitionSpec as P

FIRST_DILATION = 512
SECOND_DILATION = 1024
BF = jnp.bfloat16
F32 = jnp.float32
ZH, NY, NC, ZL, NX = 2, 8, 2, 4, 4
NS = ZL * NX
NZ = ZH * ZL
C = 512
R = 512
PARTS = 1
M = R // PARTS
SUB = M // NS
S1 = FIRST_DILATION // NS // PARTS
S2 = SECOND_DILATION // NS // PARTS
HALF = C // NC
YW = HALF // NY
ZW = YW // ZH
XW = C // NX


def silu_grad(value):
    sigma = jax.nn.sigmoid(value)
    return sigma * (1.0 + value * (1.0 - sigma))


def nn(a, b):
    return jnp.dot(a, b, preferred_element_type=F32)


def nt(a, b):
    return lax.dot_general(a, b, (((1,), (1,)), ((), ())), preferred_element_type=F32)


def kernel(
    frames, cot, first, second, perm_i, perm_o,
    out, grads,
    fp, hp, fq, hq, d1, d2, cots, g1, g2, hg, ig, tt,
    acc, other, got, s0, sx, rx, sy, ry, s2, rz,
    w1, w2, w1t, w2t, sem_l,
    sem_f, sem_c, sem_g, sem_w, sem_x, sem_y, sem_z,
):
    h = lax.axis_index("hosp")
    s = lax.axis_index("seq")
    core = lax.rem(h, NC)
    y = lax.rem(lax.div(h, NC), NY)
    zh = lax.div(h, NC * NY)
    x = lax.rem(s, NX)
    zl = lax.div(s, NX)
    z = zh * ZL + zl

    def seq_dev(t):
        return (h, t)

    def x_dev(t):
        return (h, zl * NX + t)

    def y_dev(t):
        return ((zh * NY + t) * NC + core, s)

    def z_dev(t):
        return ((lax.div(t, ZL) * NY + y) * NC + core, lax.rem(t, ZL) * NX + x)

    partner = (h + 1 - 2 * core, s)
    loads = [
        pltpu.make_async_copy(src, dst, sem_l.at[i])
        for i, (src, dst) in enumerate(
            ((first, w1), (second, w2))
        )
    ]

    def at_part(t):
        return pl.ds(pl.multiple_of(t * SUB, SUB), SUB)

    def at_pad(t):
        return pl.ds(pl.multiple_of(2 * S1 + t * SUB, SUB), SUB)

    def at_full(p):
        return lambda t: pl.ds(pl.multiple_of(t * (PARTS * SUB) + p * SUB, SUB), SUB)

    own_f = [
        pltpu.make_async_copy(
            frames.at[at_full(p)(s)], fp.at[p, at_pad(s)], sem_l.at[4 + p]
        )
        for p in range(PARTS)
    ]
    own_c = [
        pltpu.make_async_copy(
            cot.at[at_full(p)(s)], cots.at[p, at_part(s)], sem_l.at[6 + p]
        )
        for p in range(PARTS)
    ]
    barrier = pltpu.get_barrier_semaphore()

    def greet(dev):
        pl.semaphore_signal(barrier, inc=1, device_id=dev, device_id_type=pl.DeviceIdType.MESH)

    def loop(first, last, body):
        def step(r, carry):
            body(r)
            return carry

        lax.fori_loop(first, last, step, 0)

    loop(1, NS, lambda r: greet(seq_dev(lax.rem(s + r, NS))))
    loop(1, NY, lambda r: greet(y_dev(lax.rem(y + r, NY))))
    loop(0, ZL, lambda r: greet(z_dev((1 - zh) * ZL + r)))
    greet(partner)
    pl.semaphore_wait(barrier, NS - 1 + NY - 1 + ZL + 1)

    class Exchange:
        def __init__(self, n, me, dev, src, dst, sem):
            self.n, self.me, self.dev, self.src, self.dst, self.sem = n, me, dev, src, dst, sem

        def copy(self, r, to, slot):
            return pltpu.make_async_remote_copy(
                src_ref=self.src(to), dst_ref=self.dst(slot),
                send_sem=self.sem.at[0, r], recv_sem=self.sem.at[1, r],
                device_id=self.dev(to), device_id_type=pl.DeviceIdType.MESH,
            )

        def push(self):
            def body(r):
                self.copy(r, lax.rem(self.me + r, self.n), self.me).start()

            loop(self.n // 2, self.n, body)
            loop(1, self.n // 2, body)

        def land(self):
            def body(r):
                slot = lax.rem(self.me + self.n - r, self.n)
                self.copy(r, lax.rem(self.me + r, self.n), slot).wait_recv()

            loop(1, self.n, body)

        def sent(self):
            loop(1, self.n, lambda r: self.copy(r, lax.rem(self.me + r, self.n), self.me).wait_send())

    ex_f = [
        Exchange(NS, s, seq_dev, lambda t, p=p: frames.at[at_full(p)(t)],
                 lambda t, p=p: fp.at[p, at_pad(t)], sem_f.at[p])
        for p in range(PARTS)
    ]
    ex_c = [
        Exchange(NS, s, seq_dev, lambda t, p=p: cot.at[at_full(p)(t)],
                 lambda t, p=p: cots.at[p, at_part(t)], sem_c.at[p])
        for p in range(PARTS)
    ]
    ex_g = [
        Exchange(NS, s, seq_dev, lambda t, p=p: ig.at[p, at_part(t)],
                 lambda t, p=p: out.at[at_full(p)(t)], sem_g.at[p])
        for p in range(PARTS)
    ]

    def at_y(t):
        return pl.ds(pl.multiple_of(t * YW, YW), YW)

    def at_x(t):
        return pl.ds(pl.multiple_of(t * XW, XW), XW)

    def at_z(t):
        return pl.ds(pl.multiple_of(lax.div(t, ZL) * ZW, ZW), ZW)

    def y_stage(layer):
        return Exchange(
            NY, y, y_dev, lambda t: sy.at[layer, :, at_y(t), :], lambda t: ry.at[layer, t],
            sem_y.at[layer],
        )

    ex_y = (y_stage(0), y_stage(1))
    ex_z = Exchange(NZ, z, z_dev, lambda t: s2.at[:, at_z(t), :], lambda t: rz.at[t], sem_z)

    for p in range(PARTS):
        ex_f[p].push()
        ex_c[p].push()
        if p == 0:
            for load in (*loads, *own_f, *own_c):
                load.start()

    for p in range(PARTS):
        fp[p, 0 : 2 * S1, :] = jnp.zeros((2 * S1, C), BF)
        fq[p, 0 : 2 * S1, :] = jnp.zeros((2 * S1, C), BF)
        hp[p, 0 : 2 * S2, :] = jnp.zeros((2 * S2, C), BF)
        hq[p, 0 : 2 * S2, :] = jnp.zeros((2 * S2, C), BF)
        d1[p, M : M + 2 * S1, :] = jnp.zeros((2 * S1, C), BF)
        d2[p, M : M + 2 * S2, :] = jnp.zeros((2 * S2, C), BF)

    def behind(ref, p, shift):
        return jnp.concatenate([ref[p, j * shift : j * shift + M, :] for j in (2, 1, 0)], axis=1)

    def beyond(ref, p, shift):
        return jnp.concatenate([ref[p, j * shift : j * shift + M, :] for j in (0, 1, 2)], axis=1)

    def forward(p):
        own_f[p].wait()
        ex_f[p].land()
        here = fp[p, 2 * S1 :, :]
        pre = nn(behind(fp, p, S1), w1[...])
        sigma = jax.nn.sigmoid(pre)
        g1[p] = sigma * (1.0 + pre * (1.0 - sigma))
        hp[p, 2 * S2 :, :] = (here.astype(F32) + pre * sigma).astype(BF)
        g2[p] = silu_grad(nn(behind(hp, p, S2), w2[...]))
        fq[p, 2 * S1 :, :] = nn(here, perm_i[...]).astype(BF)
        hq[p, 2 * S2 :, :] = nn(hp[p, 2 * S2 :, :], perm_i[...]).astype(BF)

    def second_delta(p):
        own_c[p].wait()
        ex_c[p].land()
        d2[p, 0:M, :] = (cots[p].astype(F32) * g2[p]).astype(BF)

    def first_delta(p):
        value = cots[p].astype(F32) + nn(beyond(d2, p, S2), w2t[...])
        hg[p] = value
        d1[p, 0:M, :] = (value * g1[p]).astype(BF)

    def input_grad(p):
        ig[p] = (hg[p] + nn(beyond(d1, p, S1), w1t[...])).astype(BF)

    def send_grad(p):
        ex_g[p].push()
        out[at_full(p)(s), :] = ig[p, at_part(s), :]

    def swap(layer, k):
        return pltpu.make_async_remote_copy(
            src_ref=other.at[layer, k], dst_ref=got.at[layer, k],
            send_sem=sem_w.at[0, layer, k], recv_sem=sem_w.at[1, layer, k],
            device_id=partner, device_id_type=pl.DeviceIdType.MESH,
        )

    def taps(source, p, k, shift):
        return source[p, pl.ds(pl.multiple_of((2 - k) * shift, SUB), M), :]

    def turn(delta, p):
        tt[...] = nt(perm_o[...], delta[p, 0:M, :]).astype(BF)

    def terms(layer, delta, source, shift, between):
        turn(delta, 0)

        def theirs(k):
            value = nn(tt[HALF:, :], taps(source, 0, k, shift))
            other[layer, k] = value.astype(BF)
            swap(layer, k).start()

        loop(0, 3, theirs)
        between()

        def ours(k):
            acc[layer, k] = nn(tt[:HALF, :], taps(source, 0, k, shift))

        loop(0, 3, ours)

    def pair_sum(layer):
        def one(k):
            swap(layer, k).wait_recv()
            s0[layer, k] = (acc[layer, k] + got[layer, k].astype(F32)).astype(BF)

        loop(0, 3, one)

    right, left, far = (lax.rem(x + d, NX) for d in (1, NX - 1, NX // 2))
    low, high = pl.ds(0, HALF // 2), pl.ds(HALF // 2, HALF // 2)

    def piece(layer, part, to):
        return s0.at[layer, :, part, at_x(to)]

    def hop(layer, i):
        source = (
            lambda: piece(layer, low, far), lambda: piece(layer, high, far),
            lambda: piece(layer, high, right), lambda: piece(layer, low, left),
            lambda: sx.at[layer, 0], lambda: sx.at[layer, 1],
        )[i]()
        return pltpu.make_async_remote_copy(
            src_ref=source, dst_ref=rx.at[layer, i],
            send_sem=sem_x.at[0, layer, i], recv_sem=sem_x.at[1, layer, i],
            device_id=x_dev(left if i % 2 else right), device_id_type=pl.DeviceIdType.MESH,
        )

    def x_first(layer):
        for i in range(4):
            hop(layer, i).start()

    def x_merge(layer):
        for i, own in ((0, piece(layer, low, right)), (1, piece(layer, high, left))):
            hop(layer, i).wait_recv()
            sx[layer, i] = (own[...].astype(F32) + rx[layer, i].astype(F32)).astype(BF)
            hop(layer, 4 + i).start()

    def x_sum(layer):
        for i in (2, 3, 4, 5):
            hop(layer, i).wait_recv()
        for part, a, b in ((low, 3, 4), (high, 2, 5)):
            total = (
                piece(layer, part, x)[...].astype(F32) + rx[layer, a].astype(F32)
                + rx[layer, b].astype(F32)
            )
            sy[layer, :, part, :] = total.astype(BF)
        ex_y[layer].push()

    unit = lax.broadcasted_iota(jnp.int32, (C, C), 0) == lax.broadcasted_iota(jnp.int32, (C, C), 1)
    unit = unit.astype(F32).astype(BF)
    for load, w, wt in ((loads[0], w1, w1t), (loads[1], w2, w2t)):
        load.wait()
        for k in range(3):
            wt[k * C : (k + 1) * C, :] = nt(unit, w[k * C : (k + 1) * C, :]).astype(BF)

    forward(0)
    second_delta(0)
    terms(1, d2, hq, S2, lambda: None)
    first_delta(0)
    pair_sum(1)
    x_first(1)
    terms(0, d1, fq, S1, lambda: x_merge(1))
    pair_sum(0)
    x_first(0)
    x_sum(1)
    input_grad(0)
    x_merge(0)
    send_grad(0)

    def gather(ex, own, n, me):
        ex.dst(me)[...] = own
        ex.land()
        ref = ex.dst
        total = ref(0)[...].astype(F32)
        for t in range(1, n):
            total = total + ref(t)[...].astype(F32)
        return total

    x_sum(0)
    s2[3:6] = gather(ex_y[1], sy[1, :, at_y(y), :], NY, y).astype(BF)
    s2[0:3] = gather(ex_y[0], sy[0, :, at_y(y), :], NY, y).astype(BF)
    ex_z.push()
    grads[...] = gather(ex_z, s2[:, at_z(z), :], NZ, z)
    ex_g[0].land()

    for ex in (*ex_f, *ex_c, *ex_g, *ex_y, ex_z):
        ex.sent()
    for i in range(6):
        hop(0, i).wait_send()
        hop(1, i).wait_send()
    loop(0, 3, lambda k: swap(0, k).wait_send())
    loop(0, 3, lambda k: swap(1, k).wait_send())


def per_device(frames, cotangent, first_filter, second_filter):
    core = lax.axis_index("hosp") % NC
    zl = lax.axis_index("seq") // NX
    a = jnp.arange(C)
    width = C // NS
    i_from = ((a // width) % ZL) * (NX * width) + (a // (ZL * width)) * width + a % width
    perm_i = (a[:, None] == i_from[None, :]).astype(BF)
    owner = jnp.where(a < HALF, core, 1 - core)
    b = a % HALF
    o_from = ((b // ZW) % ZH) * (NY * NC * ZW) + (b // YW) * (NC * ZW) + owner * ZW + b % ZW
    perm_o = (o_from[:, None] == a[None, :]).astype(BF)

    vmem = pl.BlockSpec(memory_space=pltpu.VMEM)
    hbm = pl.BlockSpec(memory_space=pltpu.HBM)
    dma = pltpu.SemaphoreType.DMA
    out, grads = pl.pallas_call(
        kernel,
        out_shape=(
            jax.ShapeDtypeStruct((R, C), BF),
            jax.ShapeDtypeStruct((6, ZW, XW), F32),
        ),
        in_specs=[hbm] * 4 + [vmem] * 2,
        out_specs=(vmem, vmem),
        scratch_shapes=[
            pltpu.VMEM((PARTS, M + 2 * S1, C), BF),
            pltpu.VMEM((PARTS, M + 2 * S2, C), BF),
            pltpu.VMEM((PARTS, M + 2 * S1, C), BF),
            pltpu.VMEM((PARTS, M + 2 * S2, C), BF),
            pltpu.VMEM((PARTS, M + 2 * S1, C), BF),
            pltpu.VMEM((PARTS, M + 2 * S2, C), BF),
            pltpu.VMEM((PARTS, M, C), BF),
            pltpu.VMEM((PARTS, M, C), F32),
            pltpu.VMEM((PARTS, M, C), F32),
            pltpu.VMEM((PARTS, M, C), F32),
            pltpu.VMEM((PARTS, M, C), BF),
            pltpu.VMEM((C, M), BF),
            pltpu.VMEM((2, 3, HALF, C), F32),
            pltpu.VMEM((2, 3, HALF, C), BF),
            pltpu.VMEM((2, 3, HALF, C), BF),
            pltpu.VMEM((2, 3, HALF, C), BF),
            pltpu.VMEM((2, 2, 3, HALF // 2, XW), BF),
            pltpu.VMEM((2, 6, 3, HALF // 2, XW), BF),
            pltpu.VMEM((2, 3, HALF, XW), BF),
            pltpu.VMEM((2, NY, 3, YW, XW), BF),
            pltpu.VMEM((6, YW, XW), BF),
            pltpu.VMEM((NZ, 6, ZW, XW), BF),
            pltpu.VMEM((3 * C, C), BF),
            pltpu.VMEM((3 * C, C), BF),
            pltpu.VMEM((3 * C, C), BF),
            pltpu.VMEM((3 * C, C), BF),
            dma((8,)),
            dma((PARTS, 2, NS)),
            dma((PARTS, 2, NS)),
            dma((PARTS, 2, NS)),
            dma((2, 2, 3)),
            dma((2, 2, 6)),
            dma((2, 2, NY)),
            dma((2, NZ)),
        ],
        compiler_params=pltpu.CompilerParams(
            collective_id=0, has_side_effects=True, vmem_limit_bytes=56 * 1024 * 1024
        ),
    )(
        frames[0], cotangent[0],
        first_filter.reshape(3 * C, C), second_filter.reshape(3 * C, C),
        perm_i, perm_o,
    )
    scale = 1.0 / math.sqrt(lax.axis_size("hosp") * R * lax.axis_size("seq"))
    own = lax.dynamic_slice_in_dim(grads, zl * width, width, axis=2) * scale
    own = own.transpose(2, 0, 1)
    return (out[None], own[:, :3], own[:, 3:])


def solution(mesh):
    in_specs = (P("hosp", "seq", None), P("hosp", "seq", None), P(), P())
    out_specs = (P("hosp", "seq", None), P("seq", None, "hosp"), P("seq", None, "hosp"))
    return jax.shard_map(
        per_device, mesh=mesh, in_specs=in_specs, out_specs=out_specs, check_vma=False
    )
```
